32 devices in a mesh: replica: 2 (over x), fsdp: 16 (over z, y, core).
Axes of the slice: x: 2, y: 2, z: 4, core: 2. Of those that a mesh axis runs over, the one named last changes fastest.
Arguments:
- tokens: bfloat16 [4096, 768], P(('replica', 'fsdp')), may hold values from -6 to 6
- prefix_length: int32 [32], P(('replica', 'fsdp')), may hold values from 12 to 64
- output_cotangent: bfloat16 [4096, 768], P(('replica', 'fsdp')), may hold values from -6 to 6
- first_gain: bfloat16 [768], P('fsdp'), may hold values from 0.5 to 1.5
- first_shift: bfloat16 [768], P('fsdp'), may hold values from -3 to 3
- query_weight: bfloat16 [768, 768], P('fsdp'), may hold values from -0.21875 to 0.21875
- query_bias: bfloat16 [768], P('fsdp'), may hold values from -3 to 3
- pair_weight: bfloat16 [768, 128], P('fsdp'), may hold values from -0.21875 to 0.21875
- value_bias: bfloat16 [64], P('fsdp'), may hold values from -3 to 3
- output_weight: bfloat16 [768, 768], P('fsdp'), may hold values from -0.875 to 0.875
- output_bias: bfloat16 [768], P('fsdp'), may hold values from -3 to 3
- second_gain: bfloat16 [768], P('fsdp'), may hold values from 0.5 to 1.5
- second_shift: bfloat16 [768], P('fsdp'), may hold values from -3 to 3
- up_weight: bfloat16 [768, 3072], P('fsdp'), may hold values from -0.21875 to 0.21875
- up_bias: bfloat16 [3072], P('fsdp'), may hold values from -3 to 3
- down_weight: bfloat16 [3072, 768], P('fsdp'), may hold values from -0.109375 to 0.109375
- down_bias: bfloat16 [768], P('fsdp'), may hold values from -3 to 3
Outputs:
- layer_output: bfloat16 [4096, 768], P(('replica', 'fsdp'))
- input_gradient: bfloat16 [4096, 768], P(('replica', 'fsdp'))
- first_gain_gradient: float32 [768], P('fsdp')
- first_shift_gradient: float32 [768], P('fsdp')
- query_weight_gradient: float32 [768, 768], P('fsdp')
- query_bias_gradient: float32 [768], P('fsdp')
- pair_weight_gradient: float32 [768, 128], P('fsdp')
- value_bias_gradient: float32 [64], P('fsdp')
- output_weight_gradient: float32 [768, 768], P('fsdp')
- output_bias_gradient: float32 [768], P('fsdp')
- second_gain_gradient: float32 [768], P('fsdp')
- second_shift_gradient: float32 [768], P('fsdp')
- up_weight_gradient: float32 [768, 3072], P('fsdp')
- up_bias_gradient: float32 [3072], P('fsdp')
- down_weight_gradient: float32 [3072, 768], P('fsdp')
- down_bias_gradient: float32 [768], P('fsdp')
The draws below stay inside these ranges and needn't reach their ends.
All inputs are finite; a program needn't handle non-finite values.
Results may differ from the reference program's by a relative error of at most 0.014.
Values may be sent and summed in bfloat16 or wider, within the bound.
No kernel may reach another device: no remote copies, remote signals or barrier semaphores. Data moves between devices by JAX's collectives and lax.ppermute only.
A program may use at most 128 MiB of HBM per device.

```python
import jax
import jax.numpy as jnp
from jax import lax

D = 768
HEADS = 12
HD = 64
FF = 3072
SEQ_LEN = 128
SEQS = 32
TOKENS = 4096


def draw_prefix_length(key, part):
    least = max(1, SEQ_LEN // 10)
    most = SEQ_LEN // 2
    values = jax.random.randint(jax.random.fold_in(key, 11), (SEQS,), least, most + 1)
    first_pick = jax.random.randint(jax.random.fold_in(key, 12), (), 0, SEQS)
    offset_pick = jax.random.randint(jax.random.fold_in(key, 13), (), 0, SEQS - 1)
    second_pick = (first_pick + 1 + offset_pick) % SEQS
    position = jnp.arange(SEQS)
    values = jnp.where(position == first_pick, most, values)
    values = jnp.where(position == second_pick, least, values)
    return values.astype(jnp.int32)


def strengthened(array, key, source, target, parts, factor):
    def block_of(dim):
        return (jnp.arange(array.shape[dim]) // (array.shape[dim] // parts)).reshape((-1,) + (1,) * (array.ndim - 1 - dim))

    one_side = jax.random.permutation(key, parts)[block_of(target)]
    second = (block_of(target) + parts // 2) % parts
    return jnp.where((block_of(source) == one_side) | (block_of(source) == second), factor * array, array)


def steps_of(own_key, dims, pieces, low, largest):
    loudness, own = 1.0, jax.random.fold_in(own_key, 6)
    for dim, parts in pieces:
        heights = jnp.exp(jax.random.uniform(jax.random.fold_in(own, dim), (parts,), jnp.float32, low / len(pieces), largest / len(pieces)))
        loudness = loudness * jnp.repeat(heights, dims[dim] // parts).reshape([-1 if axis == dim else 1 for axis in range(len(dims))])
    return loudness


def scatter_about(key, dims, deviation, most, cuts=(), dtype=jnp.bfloat16):
    values = jax.random.normal(key, dims, jnp.float32) * deviation
    if len(cuts) > 0:
        values = steps_of(key, dims, cuts, -0.22, 0.18) * values
    return jnp.clip(values, min=-most, max=most).astype(dtype)


def bell_draw_with(rng, dims, scale, bound, pieces, heavy, dtype=jnp.bfloat16):
    values = scale * jax.random.normal(rng, dims, jnp.float32)
    if pieces:
        values = values * steps_of(rng, dims, pieces, -0.22, 0.18)
    return jnp.clip(strengthened(values, jax.random.fold_in(rng, 3), *heavy), -bound, bound).astype(dtype)


def setup_inputs(seed: int = 0) -> dict:
    key_of = jax.random.split(jax.random.key(seed), 18)
    tokens = bell_draw_with(key_of[0], (TOKENS, D), 1.0, 6.0, ((0, 32),), (0, 1, 32, 2.75))
    prefix_length = draw_prefix_length(jax.random.fold_in(key_of[17], 71), 0)
    output_cotangent = scatter_about(key_of[2], (TOKENS, D), 1.0, 6.0, ((0, 32),))
    first_gain = jnp.clip(1.0 + 0.1 * jax.random.normal(key_of[3], (D,), jnp.float32), 0.5, 1.5).astype(jnp.bfloat16)
    first_shift = scatter_about(key_of[4], (D,), 0.5, 3.0, ((0, 16),))
    query_weight = scatter_about(key_of[5], (D, D), D ** -0.5, 0.21875, ((0, 16),))
    query_bias = scatter_about(key_of[6], (D,), 0.5, 3.0, ((0, 16),))
    pair_weight = scatter_about(key_of[7], (D, 2 * HD), D ** -0.5, 0.21875, ((0, 16),))
    value_bias = scatter_about(key_of[8], (HD,), 0.5, 3.0, ((0, 16),))
    output_weight = scatter_about(key_of[9], (D, D), (D // 16) ** -0.5, 0.875, ((0, 16),))
    output_bias = scatter_about(key_of[10], (D,), 0.5, 3.0, ((0, 16),))
    second_gain = jnp.clip(1.0 + 0.1 * jax.random.normal(key_of[11], (D,), jnp.float32), 0.5, 1.5).astype(jnp.bfloat16)
    second_shift = scatter_about(key_of[12], (D,), 0.5, 3.0, ((0, 16),))
    up_weight = scatter_about(key_of[13], (D, FF), D ** -0.5, 0.21875, ((0, 16),))
    up_bias = scatter_about(key_of[14], (FF,), 0.5, 3.0, ((0, 16),))
    down_weight = scatter_about(key_of[15], (FF, D), FF ** -0.5, 0.109375, ((0, 16),))
    down_bias = scatter_about(key_of[16], (D,), 0.5, 3.0, ((0, 16),))
    return dict(tokens=tokens, prefix_length=prefix_length, output_cotangent=output_cotangent, first_gain=first_gain, first_shift=first_shift, query_weight=query_weight, query_bias=query_bias, pair_weight=pair_weight, value_bias=value_bias, output_weight=output_weight, output_bias=output_bias, second_gain=second_gain, second_shift=second_shift, up_weight=up_weight, up_bias=up_bias, down_weight=down_weight, down_bias=down_bias)


@jax.custom_vjp
def low(v):
    return lax.optimization_barrier(v.astype(jnp.bfloat16)).astype(jnp.float32)

@jax.custom_vjp
def low_back(v):
    return v

def low_keep(v):
    return (low(v), None)

def low_pass(kept, grad):
    return (grad,)

def back_keep(v):
    return (v, None)

def back_low(kept, grad):
    return (low(grad),)
low.defvjp(low_keep, low_pass)
low_back.defvjp(back_keep, back_low)
EPSILON = 1e-05
NEGATIVE = -1e+30
PRECISE = lax.Precision.HIGHEST

def layer_norm(values, gain, shift):
    center = values - lax.optimization_barrier(jnp.mean(values, axis=-1, keepdims=True))
    spread = lax.optimization_barrier(jnp.mean(center * center, axis=-1, keepdims=True))
    return center * lax.rsqrt(spread + EPSILON) * gain + shift

def product(left, right):
    return jnp.dot(left, right, precision=PRECISE)

def visible(length, prefix):
    row_index = lax.broadcasted_iota(jnp.int32, (length, length), 0)
    col_index = lax.broadcasted_iota(jnp.int32, (length, length), 1)
    return (col_index <= row_index) | (col_index < prefix)

def forward(inputs, prefix, params):
    first_gain, first_shift, query_weight, query_bias, pair_weight, value_bias, output_weight, output_bias, second_gain, second_shift, up_weight, up_bias, down_weight, down_bias = params
    length = inputs.shape[0]
    query_scale = HD ** (-0.5)
    normed = low(layer_norm(inputs, first_gain, first_shift))
    query_rows = low(low_back(product(normed, query_weight) + query_bias) * query_scale)
    pair_rows = product(normed, pair_weight)
    key_rows = low_back(low(pair_rows[:, :HD]))
    value_rows = low_back(low(pair_rows[:, HD:] + value_bias))
    head_rows = query_rows.reshape(length, HEADS, HD)
    score_rows = low_back(jnp.einsum('qhd,kd->hqk', head_rows, key_rows, precision=PRECISE))
    score_rows = jnp.where(visible(length, prefix)[None], score_rows, NEGATIVE)
    top_score = lax.optimization_barrier(jnp.max(score_rows, axis=-1, keepdims=True))
    exponent = jnp.exp(score_rows - top_score)
    soft_weights = low(exponent / lax.optimization_barrier(jnp.sum(exponent, axis=-1, keepdims=True)))
    mixed_rows = jnp.einsum('hqk,kd->qhd', soft_weights, value_rows, precision=PRECISE).reshape(length, D)
    mixed_rows = low_back(low(mixed_rows))
    branch = low_back(product(mixed_rows, output_weight) + output_bias)
    middle = inputs + branch
    second_normed = low(layer_norm(middle, second_gain, second_shift))
    upper_rows = low_back(product(second_normed, up_weight) + up_bias)
    active = low(jax.nn.gelu(upper_rows, approximate=True))
    return middle + product(active, down_weight) + down_bias

def reference(tokens, prefix_length, output_cotangent, first_gain, first_shift, query_weight, query_bias, pair_weight, value_bias, output_weight, output_bias, second_gain, second_shift, up_weight, up_bias, down_weight, down_bias):
    params = tuple((entry.astype(jnp.float32) for entry in (first_gain, first_shift, query_weight, query_bias, pair_weight, value_bias, output_weight, output_bias, second_gain, second_shift, up_weight, up_bias, down_weight, down_bias)))
    inputs_all = tokens.astype(jnp.float32).reshape(SEQS, SEQ_LEN, D)
    cotangents = output_cotangent.astype(jnp.float32).reshape(SEQS, SEQ_LEN, D)

    def one_sequence(running, sequence_item):
        inputs, prefix, cotangent = sequence_item
        result, pullback = jax.vjp(lambda values, weights: forward(values, prefix, weights), inputs, params)
        input_grad, param_grads = pullback(cotangent)
        running = jax.tree.map(lambda left, right: left + right, running, param_grads)
        return (running, (result, input_grad))
    initial = jax.tree.map(jnp.zeros_like, params)
    totals, (results, input_grads) = lax.scan(one_sequence, initial, (inputs_all, prefix_length, cotangents))
    return (results.reshape(TOKENS, D).astype(jnp.bfloat16), input_grads.reshape(TOKENS, D).astype(jnp.bfloat16), totals[0], totals[1], totals[2], totals[3], totals[4], totals[5], totals[6], totals[7], totals[8], totals[9], totals[10], totals[11], totals[12], totals[13])
```

```python
from functools import partial

import jax
import jax.numpy as jnp
from jax import lax
from jax.sharding import PartitionSpec as P

D = 768
HEADS = 12
HD = 64
FF = 3072

EPSILON = 1e-05
NEGATIVE = -1e30
AXES = ("replica", "fsdp")
LOW = jnp.bfloat16
HIGH = jnp.float32


def layer_norm(values, gain, shift):
    center = values - jnp.mean(values, axis=-1, keepdims=True)
    spread = jnp.mean(center * center, axis=-1, keepdims=True)
    return center * lax.rsqrt(spread + EPSILON) * gain + shift


def along(left, right):
    return jnp.dot(left, right, preferred_element_type=HIGH)


def across(left, right):
    return lax.dot_general(
        left, right, (((0,), (0,)), ((), ())), preferred_element_type=HIGH
    )


def against(left, right):
    return lax.dot_general(
        left, right, (((1,), (1,)), ((), ())), preferred_element_type=HIGH
    )


def visible(length, prefix):
    row_index = lax.broadcasted_iota(jnp.int32, (length, length), 0)
    col_index = lax.broadcasted_iota(jnp.int32, (length, length), 1)
    return (col_index <= row_index) | (col_index < prefix)


class Links:
    def __init__(self, replicas, shards):
        self.replicas = replicas
        self.shards = shards
        self.chips = shards // 2
        dims = []
        stride = 1
        while stride < self.chips:
            size = 2 if not dims and self.chips == 8 else min(4, self.chips // stride)
            dims.append((stride, size))
            stride *= size
        self.dims = dims[::-1]

    def flip(self, value, replica=0, shard=0):
        pairs = [
            (r * self.shards + f, (r ^ replica) * self.shards + (f ^ shard))
            for r in range(self.replicas)
            for f in range(self.shards)
        ]
        return lax.ppermute(value, AXES, pairs)

    def sibling(self, value):
        return self.flip(value, shard=1)

    def mirror(self, value):
        return self.flip(value, replica=1)

    def gather(self, block):
        have = {0: block}
        for stride, size in self.dims:
            new = {}
            for away, held in have.items():
                for step in range(1, size):
                    new[away ^ (step * stride)] = self.flip(held, shard=2 * step * stride)
            have.update(new)
        return have

    def scatter(self, total, chip):
        shape = tuple(size for _, size in self.dims)
        rest = total.shape[1:]
        total = total.reshape(shape + rest)
        for stride, size in self.dims[::-1]:
            axis = total.ndim - len(rest) - 1
            place = (chip // stride) % size

            def part(at):
                return lax.dynamic_index_in_dim(total, at, axis, keepdims=False)

            own = part(place).astype(HIGH)
            for step in range(1, size):
                own = own + self.flip(part(place ^ step).astype(LOW), shard=2 * step * stride).astype(HIGH)
            total = own
        return total


def placed(blocks, chip, count):
    shape = blocks[0].shape
    out = jnp.zeros((count,) + shape, blocks[0].dtype)
    for away, block in blocks.items():
        out = lax.dynamic_update_slice(out, block[None], (chip ^ away,) + (0,) * len(shape))
    return out


def ordered(mine, other, bit):
    both = jnp.stack([mine, other])
    turned = jnp.stack([other, mine])
    return jnp.where(bit == 0, both, turned)


def on_device(
    links,
    tokens,
    prefix_length,
    output_cotangent,
    first_gain,
    first_shift,
    query_weight,
    query_bias,
    pair_weight,
    value_bias,
    output_weight,
    output_bias,
    second_gain,
    second_shift,
    up_weight,
    up_bias,
    down_weight,
    down_bias,
):
    length = tokens.shape[0]
    query_scale = HD ** (-0.5)
    chips = links.chips
    shards = links.shards
    replica = lax.axis_index("replica")
    shard = lax.axis_index("fsdp")
    chip = shard // 2
    core = shard % 2
    rows = query_weight.shape[0]
    wide = down_weight.shape[0]
    half = wide // 2
    few = value_bias.shape[0]
    stack = wide // rows

    vector_columns = jnp.concatenate(
        [
            jnp.stack([first_gain, first_shift, query_bias, output_bias, second_gain, second_shift, down_bias], axis=1),
            up_bias.reshape(stack, rows).T,
            jnp.pad(value_bias, (0, rows - few))[:, None],
        ],
        axis=1,
    )
    vectors = vector_columns.shape[1]
    vector_columns = jnp.pad(vector_columns, ((0, 0), (0, 128 - vectors)))
    attention_block = jnp.concatenate([query_weight, output_weight, pair_weight, vector_columns], axis=1)
    attention_here = placed(links.gather(attention_block), chip, chips)
    attention_there = links.sibling(attention_here)
    attention_all = jnp.where(
        core == 0,
        jnp.stack([attention_here, attention_there], axis=1),
        jnp.stack([attention_there, attention_here], axis=1),
    ).reshape(shards * rows, attention_block.shape[1])
    query_full = attention_all[:, :D]
    output_full = attention_all[:, D : 2 * D]
    pair_full = attention_all[:, 2 * D : 2 * D + 2 * HD]
    vector_full = attention_all[:, 2 * D + 2 * HD :].T.astype(HIGH)
    gain_one, shift_one, query_bias_full, output_bias_full, gain_two, shift_two, down_bias_full = vector_full[:7]
    up_bias_full = vector_full[7 : 7 + stack].reshape(stack, shards, rows).transpose(1, 0, 2).reshape(FF)
    value_bias_full = vector_full[7 + stack].reshape(shards, rows)[:, :few].reshape(HD)

    up_view = up_weight.reshape(rows, chips, 2, 2, half)

    def columns_of(which):
        taken = lax.dynamic_index_in_dim(up_view, which, 2, keepdims=False)
        return lax.dynamic_index_in_dim(taken, replica, 2, keepdims=False).reshape(rows, chips * half)

    up_pair = ordered(columns_of(core), links.sibling(columns_of(1 - core)), core).reshape(2 * rows, chips * half)
    down_half = lax.dynamic_slice_in_dim(down_weight, replica * half, half, axis=0)
    forward_blocks = links.gather(jnp.stack([up_pair.reshape(half, D), down_half]))
    forward_all = placed(forward_blocks, chip, chips)
    up_part = forward_all[:, 0].reshape(D, chips * half)
    down_part = forward_all[:, 1].reshape(chips * half, D)
    up_bias_part = lax.dynamic_index_in_dim(
        lax.dynamic_index_in_dim(up_bias_full.reshape(chips, 2, 2, half), core, 1, keepdims=False),
        replica,
        1,
        keepdims=False,
    ).reshape(chips * half)

    def spread(value):
        near = jnp.concatenate([value, links.mirror(value)], axis=0)
        return jnp.concatenate([near, links.sibling(near)], axis=0)

    def collect(parts):
        near = parts[: 2 * length] + links.sibling(parts[2 * length :].astype(LOW)).astype(HIGH)
        return near[:length] + links.mirror(near[length:].astype(LOW)).astype(HIGH)

    cotangent_rows = spread(output_cotangent)

    inputs = tokens.astype(HIGH)
    prefix = prefix_length[0]
    normed_one, norm_back_one = jax.vjp(layer_norm, inputs, gain_one, shift_one)
    normed_low = normed_one.astype(LOW)
    query_rows = ((along(normed_low, query_full) + query_bias_full) * query_scale).astype(LOW)
    pair_rows = along(normed_low, pair_full)
    key_rows = pair_rows[:, :HD].astype(LOW)
    value_rows = (pair_rows[:, HD:] + value_bias_full).astype(LOW)
    head_rows = query_rows.reshape(length, HEADS, HD)
    allowed = visible(length, prefix)[None]
    score_rows = jnp.where(
        allowed,
        jnp.einsum("qhd,kd->hqk", head_rows, key_rows, preferred_element_type=HIGH),
        NEGATIVE,
    )
    top_score = jnp.max(score_rows, axis=-1, keepdims=True)
    exponent = jnp.exp(score_rows - top_score)
    row_total = jnp.sum(exponent, axis=-1, keepdims=True)
    log_total = top_score + jnp.log(row_total)
    soft_low = (exponent / row_total).astype(LOW)
    mixed_low = (
        jnp.einsum("hqk,kd->qhd", soft_low, value_rows, preferred_element_type=HIGH)
        .reshape(length, D)
        .astype(LOW)
    )
    middle = inputs + along(mixed_low, output_full) + output_bias_full
    normed_two, norm_back_two = jax.vjp(layer_norm, middle, gain_two, shift_two)
    second_low = normed_two.astype(LOW)

    second_rows = spread(second_low)
    upper_rows = along(second_rows, up_part) + up_bias_part
    active, gelu_back = jax.vjp(partial(jax.nn.gelu, approximate=True), upper_rows)
    active_low = active.astype(LOW)
    active_grad = against(cotangent_rows, down_part)
    upper_grad = gelu_back(active_grad)[0].astype(LOW)
    second_grad = collect(against(upper_grad, up_part))
    up_bias_part_grad = jnp.sum(upper_grad.astype(HIGH), axis=0)
    up_grad = across(second_rows, upper_grad).astype(LOW)
    down_grad = across(active_low, cotangent_rows).astype(LOW)
    lower_sum = collect(along(active_low, down_part))
    layer_output = (middle + lower_sum + down_bias_full).astype(LOW)

    forward_grad = links.scatter(
        jnp.stack([up_grad.reshape(chips, half, D), down_grad.reshape(chips, half, D)], axis=1), chip
    )
    up_rows = forward_grad[0].reshape(2, rows, chips * half)
    up_own = lax.dynamic_index_in_dim(up_rows, core, 0, keepdims=False)
    up_other = links.sibling(lax.dynamic_index_in_dim(up_rows, 1 - core, 0, keepdims=False).astype(LOW))
    up_cores = ordered(up_own.astype(LOW), up_other, core)
    pack = jnp.concatenate([up_cores.reshape(2 * rows, chips * half), forward_grad[1].astype(LOW)], axis=0)
    packs = ordered(pack, links.mirror(pack), replica)
    up_weight_grad = (
        packs[:, : 2 * rows]
        .reshape(2, 2, rows, chips, half)
        .transpose(2, 3, 1, 0, 4)
        .reshape(rows, FF)
        .astype(HIGH)
    )
    down_weight_grad = packs[:, 2 * rows :].reshape(wide, D).astype(HIGH)

    cotangent = output_cotangent.astype(HIGH)
    down_bias_grad = jnp.sum(cotangent, axis=0)
    middle_part, gain_two_grad, shift_two_grad = norm_back_two(second_grad)
    middle_grad = cotangent + middle_part
    branch_low = middle_grad.astype(LOW)
    output_bias_grad = jnp.sum(branch_low.astype(HIGH), axis=0)
    output_grad = across(mixed_low, branch_low)
    mixed_grad = against(branch_low, output_full).astype(LOW).reshape(length, HEADS, HD)
    soft_grad = jnp.einsum("qhd,kd->hqk", mixed_grad, value_rows, preferred_element_type=HIGH)
    soft_again = jnp.exp(score_rows - log_total)
    value_grad = jnp.einsum(
        "hqk,qhd->kd", soft_again.astype(LOW), mixed_grad, preferred_element_type=HIGH
    )
    score_grad = (
        soft_again * (soft_grad - jnp.sum(soft_again * soft_grad, axis=-1, keepdims=True))
    ).astype(LOW)
    query_grad = (
        jnp.einsum("hqk,kd->qhd", score_grad, key_rows, preferred_element_type=HIGH).reshape(length, D)
        * query_scale
    ).astype(LOW)
    key_grad = jnp.einsum("hqk,qhd->kd", score_grad, head_rows, preferred_element_type=HIGH)
    pair_grad = jnp.concatenate([key_grad, value_grad], axis=1).astype(LOW)
    query_bias_grad = jnp.sum(query_grad.astype(HIGH), axis=0)
    value_bias_grad = jnp.sum(pair_grad[:, HD:].astype(HIGH), axis=0)
    normed_grad = against(query_grad, query_full) + against(pair_grad, pair_full)
    input_part, gain_one_grad, shift_one_grad = norm_back_one(normed_grad)
    input_gradient = (middle_grad + input_part).astype(LOW)

    up_bias_grad = jnp.zeros((chips, 2, 2, half), HIGH)
    up_bias_grad = lax.dynamic_update_slice(
        up_bias_grad, up_bias_part_grad.reshape(chips, 1, 1, half), (0, core, replica, 0)
    ).reshape(shards, stack, rows)
    vector_rows = jnp.concatenate(
        [
            jnp.stack(
                [
                    gain_one_grad,
                    shift_one_grad,
                    query_bias_grad,
                    output_bias_grad,
                    gain_two_grad,
                    shift_two_grad,
                    down_bias_grad,
                ]
            ),
            up_bias_grad.transpose(1, 0, 2).reshape(stack, D),
            jnp.pad(value_bias_grad.reshape(shards, few), ((0, 0), (0, rows - few))).reshape(1, D),
        ]
    )
    vector_rows = jnp.pad(vector_rows, ((0, 128 - vectors), (0, 0)))
    attention_grad = jnp.concatenate(
        [
            across(normed_low, query_grad).astype(LOW),
            output_grad.astype(LOW),
            across(normed_low, pair_grad).astype(LOW),
            vector_rows.T.astype(LOW),
        ],
        axis=1,
    ).reshape(chips, 2, rows, attention_block.shape[1])
    grad_own = lax.dynamic_index_in_dim(attention_grad, core, 1, keepdims=False)
    grad_other = links.sibling(lax.dynamic_index_in_dim(attention_grad, 1 - core, 1, keepdims=False))
    grad_part = links.scatter(grad_own.astype(HIGH) + grad_other.astype(HIGH), chip).astype(LOW)
    grad_all = grad_part.astype(HIGH) + links.mirror(grad_part).astype(HIGH)
    vector_all = grad_all[:, 2 * D + 2 * HD :].T
    return (
        layer_output,
        input_gradient,
        vector_all[0],
        vector_all[1],
        grad_all[:, :D],
        vector_all[2],
        grad_all[:, 2 * D : 2 * D + 2 * HD],
        vector_all[7 + stack][:few],
        grad_all[:, D : 2 * D],
        vector_all[3],
        vector_all[4],
        vector_all[5],
        up_weight_grad,
        vector_all[7 : 7 + stack].reshape(wide),
        down_weight_grad,
        vector_all[6],
    )


def solution(mesh):
    links = Links(mesh.shape["replica"], mesh.shape["fsdp"])
    in_specs = (
        P(("replica", "fsdp"), None),
        P(("replica", "fsdp")),
        P(("replica", "fsdp"), None),
        P("fsdp"),
        P("fsdp"),
        P("fsdp", None),
        P("fsdp"),
        P("fsdp", None),
        P("fsdp"),
        P("fsdp", None),
        P("fsdp"),
        P("fsdp"),
        P("fsdp"),
        P("fsdp", None),
        P("fsdp"),
        P("fsdp", None),
        P("fsdp"),
    )
    out_specs = (
        P(("replica", "fsdp"), None),
        P(("replica", "fsdp"), None),
        P("fsdp"),
        P("fsdp"),
        P("fsdp", None),
        P("fsdp"),
        P("fsdp", None),
        P("fsdp"),
        P("fsdp", None),
        P("fsdp"),
        P("fsdp"),
        P("fsdp"),
        P("fsdp", None),
        P("fsdp"),
        P("fsdp", None),
        P("fsdp"),
    )
    return jax.shard_map(
        partial(on_device, links), mesh=mesh, in_specs=in_specs, out_specs=out_specs, check_vma=False
    )
```
